32 devices in a mesh: dp: 16 (over z, x, core), tensor: 2 (over y).
Axes of the slice: x: 2, y: 2, z: 4, core: 2. Of those that a mesh axis runs over, the one named last changes fastest.
Arguments:
- tokens: bfloat16 [4096, 1024], P('dp'), may hold values from -6 to 6
- cotangent: bfloat16 [4096, 1024], P('dp'), may hold values from -6 to 6
- seq_lens: int32 [64], P('dp'), may hold values from 0 to 256, as said below
- layer_norm_gain: float32 [2, 1024], replicated, may hold values from 0.1 to 1.9
- layer_norm_bias: float32 [2, 1024], replicated, may hold values from -2 to 2
- w_qkv: bfloat16 [3, 1024, 1024], P(None, 'dp', 'tensor'), may hold values from -1 to 1
- b_qv: float32 [2, 1024], P(None, 'tensor'), may hold values from -2 to 2
- w_out: bfloat16 [1024, 1024], P('dp', 'tensor'), may hold values from -0.75 to 0.75
- b_out: float32 [1024], replicated, may hold values from -2 to 2
- w_fc1: bfloat16 [1024, 4096], P('dp', 'tensor'), may hold values from -0.1875 to 0.1875
- b_fc1: float32 [4096], P('tensor'), may hold values from -3 to 3
- w_fc2: bfloat16 [1024, 4096], P('dp', 'tensor'), may hold values from -0.09375 to 0.09375
- b_fc2: float32 [1024], replicated, may hold values from -2 to 2
Outputs:
- output: bfloat16 [4096, 1024], P('dp')
- grad_tokens: float32 [4096, 1024], P('dp')
- grad_norm_gain: float32 [2, 1024], replicated
- grad_norm_bias: float32 [2, 1024], replicated
- grad_w_qkv: float32 [3, 1024, 1024], P(None, 'dp', 'tensor')
- grad_b_qv: float32 [2, 1024], P(None, 'tensor')
- grad_w_out: float32 [1024, 1024], P('dp', 'tensor')
- grad_b_out: float32 [1024], replicated
- grad_w_fc1: float32 [1024, 4096], P('dp', 'tensor')
- grad_b_fc1: float32 [4096], P('tensor')
- grad_w_fc2: float32 [1024, 4096], P('dp', 'tensor')
- grad_b_fc2: float32 [1024], replicated
The draws below stay inside these ranges and needn't reach their ends.
Inputs may be any that keep to these rules, and one draw needn't show every extreme that they name: `seq_lens`: each device's 4 lengths are whole sequences laid one after another from its first row; they sum to at most 256, and some device holds a single sequence of exactly 256 rows. Rows after a device's sequences are padding.
All inputs are finite; a program needn't handle non-finite values.
Results may differ from the reference program's by a relative error of at most 0.014.
Values may be sent and summed in bfloat16 or wider, within the bound.
A program may use at most 128 MiB of HBM per device.

```python
import jax
import jax.numpy as jnp
from jax import lax

D = 1024
HEAD_DIM = 64
FF = 4096
TOK_DEV = 256
SEQ_DEV = 4
TOKENS = 4096
SEQS = 64
N_DP = 16


def draw_seq_lens(key, part):
    device_count = SEQS // SEQ_DEV
    key_used = jax.random.fold_in(key, 11)
    key_full = jax.random.fold_in(key, 12)
    key_cuts = jax.random.fold_in(key, 13)
    used = jax.random.randint(key_used, (device_count,), TOK_DEV // 4, TOK_DEV + 1)
    full_device = jax.random.randint(key_full, (), 0, device_count)
    cuts = jax.random.randint(key_cuts, (device_count, SEQ_DEV - 1), 0, TOK_DEV + 1)
    cuts = jnp.sort(jnp.minimum(cuts, used[:, None]), axis=1)
    edges = jnp.concatenate([jnp.zeros((device_count, 1), jnp.int32), cuts.astype(jnp.int32), used[:, None].astype(jnp.int32)], axis=1)
    lengths = edges[:, 1:] - edges[:, :-1]
    single = jnp.zeros((SEQ_DEV,), jnp.int32).at[0].set(TOK_DEV)
    chosen = (jnp.arange(device_count) == full_device)[:, None]
    lengths = jnp.where(chosen, single[None, :], lengths)
    return lengths.reshape(-1).astype(jnp.int32)


def draw_w_qkv(key, part):
    key_base = jax.random.fold_in(key, 21)
    base = jax.random.normal(key_base, (3, D, D), jnp.float32) * D ** (-0.5)
    weights = base
    return jnp.clip(weights, -1.0, 1.0).astype(jnp.bfloat16)


def strengthened(drawn, stream_key, source, target, shards_of, factor):
    owner, partner = [(jnp.arange(drawn.shape[dim]) // (drawn.shape[dim] // shards_of)).reshape([-1 if axis == dim else 1 for axis in range(drawn.ndim)]) for dim in (source, target)]
    chosen = jax.random.permutation(stream_key, shards_of)[partner]
    strong = (owner == chosen) | (owner == (partner + shards_of // 2) % shards_of)
    return jnp.where(strong, factor * drawn, drawn)


def block_scale(own_key, shape, split, smallest, top_value):
    level, own = 1.0, jax.random.fold_in(own_key, 6)
    for position, parts in split:
        draws = jnp.exp(jax.random.uniform(jax.random.fold_in(own, position), (parts,), jnp.float32, smallest / len(split), top_value / len(split)))
        level = level * jnp.repeat(draws, shape[position] // parts).reshape([-1 if axis == position else 1 for axis in range(len(shape))])
    return level


def gaussian(rng, dims, width, reach, pieces=(), kind=jnp.bfloat16):
    loudness = block_scale(rng, dims, pieces, -0.22, 0.18) if pieces else 1.0
    drawn = jax.random.normal(rng, dims, jnp.float32) * width * loudness
    return jnp.minimum(jnp.maximum(drawn, -reach), reach).astype(kind)


def noise_with(rng, shape, width, most, shards, heavy, kind=jnp.bfloat16):
    drawn = width * jax.random.normal(rng, shape, jnp.float32)
    if shards:
        drawn = drawn * block_scale(rng, shape, shards, -0.22, 0.18)
    return jnp.clip(strengthened(drawn, jax.random.fold_in(rng, 3), *heavy), -most, most).astype(kind)


def setup_inputs(seed: int = 0) -> dict:
    splits = jax.random.split(jax.random.key(seed), 14)
    tokens = gaussian(splits[0], (TOKENS, D), 1.0, 6.0, ((0, 16),))
    cotangent = noise_with(splits[1], (TOKENS, D), 1.0, 6.0, ((0, 16),), (0, 1, 16, 2.0))
    seq_lens = draw_seq_lens(jax.random.fold_in(splits[13], 71), 0)
    layer_norm_gain = jnp.clip(1.0 + 0.18 * jax.random.normal(splits[3], (2, D), jnp.float32), 0.1, 1.9)
    layer_norm_bias = gaussian(splits[4], (2, D), 0.3, 2.0, (), jnp.float32)
    w_qkv = draw_w_qkv(jax.random.fold_in(splits[13], 71), 0)
    b_qv = gaussian(splits[6], (2, D), 0.3, 2.0, ((1, 2),), jnp.float32)
    w_out = gaussian(splits[7], (D, D), (D // 16) ** -0.5, 0.75, ((0, 16), (1, 2)))
    b_out = gaussian(splits[8], (D,), 0.3, 2.0, (), jnp.float32)
    w_fc1 = gaussian(splits[9], (D, FF), D ** -0.5, 0.1875, ((0, 16), (1, 2)))
    b_fc1 = gaussian(splits[10], (FF,), 0.5, 3.0, ((0, 2),), jnp.float32)
    w_fc2 = gaussian(splits[11], (D, FF), FF ** -0.5, 0.09375, ((0, 16), (1, 2)))
    b_fc2 = gaussian(splits[12], (D,), 0.3, 2.0, (), jnp.float32)
    return {"tokens": tokens, "cotangent": cotangent, "seq_lens": seq_lens, "layer_norm_gain": layer_norm_gain, "layer_norm_bias": layer_norm_bias, "w_qkv": w_qkv, "b_qv": b_qv, "w_out": w_out, "b_out": b_out, "w_fc1": w_fc1, "b_fc1": b_fc1, "w_fc2": w_fc2, "b_fc2": b_fc2}


NORM_EPS = 1e-05
GELU_COEF = 0.7978845608028654

def product(spec, left, right):
    return jnp.einsum(spec, left.astype(jnp.float32), right.astype(jnp.float32))

def seq_masks(lengths, row_count):
    ends = jnp.cumsum(lengths, dtype=jnp.int32)
    places = jnp.arange(row_count, dtype=jnp.int32)
    segment = lax.optimization_barrier(jnp.sum((places[:, None] >= ends[None, :]).astype(jnp.int32), axis=1))
    allowed = (segment[:, None] == segment[None, :]) & (places[:, None] >= places[None, :])
    live_rows = places < ends[-1]
    return (allowed, live_rows)

def layer_norm_forward(hidden, gain, shift):
    center = hidden - lax.optimization_barrier(jnp.mean(hidden, axis=-1, keepdims=True))
    inv_std = lax.rsqrt(lax.optimization_barrier(jnp.mean(center * center, axis=-1, keepdims=True)) + NORM_EPS)
    normal_x = center * inv_std
    return (normal_x * gain + shift, normal_x, inv_std)

def layer_norm_backward(grad_out, gain, normal_x, inv_std):
    scaled = grad_out * gain
    return inv_std * (scaled - lax.optimization_barrier(jnp.mean(scaled, axis=-1, keepdims=True)) - normal_x * lax.optimization_barrier(jnp.mean(scaled * normal_x, axis=-1, keepdims=True)))

def gelu_parts(pre_act):
    inner = GELU_COEF * (pre_act + 0.044715 * pre_act * pre_act * pre_act)
    tanh_val = jnp.tanh(inner)
    value = 0.5 * pre_act * (1.0 + tanh_val)
    slope = 0.5 * (1.0 + tanh_val) + 0.5 * pre_act * (1.0 - tanh_val * tanh_val) * GELU_COEF * (1.0 + 3.0 * 0.044715 * pre_act * pre_act)
    return (value, slope)

def split_heads(matrix):
    return matrix.reshape(matrix.shape[0], matrix.shape[1] // HEAD_DIM, HEAD_DIM)

def head_scores(query, key_rows, allowed):
    scores = product('qhd,khd->hqk', split_heads(query), split_heads(key_rows)) * HEAD_DIM ** (-0.5)
    return jnp.where(allowed[None], scores, -1e+30)

def attend(query, key_rows, value, allowed):
    scores = head_scores(query, key_rows, allowed)
    row_max = lax.optimization_barrier(jnp.max(scores, axis=-1, keepdims=True))
    logsum = row_max + jnp.log(lax.optimization_barrier(jnp.sum(jnp.exp(scores - row_max), axis=-1, keepdims=True)))
    weights = jnp.exp(scores - logsum).astype(jnp.bfloat16)
    mixed = product('hqk,khd->qhd', weights, split_heads(value)).astype(jnp.bfloat16)
    return (mixed.reshape(query.shape[0], -1), logsum)

def attend_back(query, key_rows, value, heads_out, d_heads, logsum, allowed):
    scores = head_scores(query, key_rows, allowed)
    probs = jnp.exp(scores - logsum)
    probs_low = probs.astype(jnp.bfloat16)
    d_split = split_heads(d_heads)
    d_prob = product('qhd,khd->hqk', d_split, split_heads(value))
    delta = lax.optimization_barrier(jnp.sum(d_split.astype(jnp.float32) * split_heads(heads_out).astype(jnp.float32), axis=-1))
    d_score = (probs * (d_prob - jnp.transpose(delta)[:, :, None]) * HEAD_DIM ** (-0.5)).astype(jnp.bfloat16)
    d_query = product('hqk,khd->qhd', d_score, split_heads(key_rows)).astype(jnp.bfloat16)
    d_key = product('hqk,qhd->khd', d_score, split_heads(query)).astype(jnp.bfloat16)
    d_value = product('hqk,qhd->khd', probs_low, d_split).astype(jnp.bfloat16)
    row_count = query.shape[0]
    return (d_query.reshape(row_count, -1), d_key.reshape(row_count, -1), d_value.reshape(row_count, -1))

def one_block(block_in, block_cot, lengths, layer_norm_gain, layer_norm_bias, w_qkv, b_qv, w_out, b_out, w_fc1, b_fc1, w_fc2, b_fc2):
    allowed, live_rows = seq_masks(lengths, block_in.shape[0])
    input_tokens = block_in.astype(jnp.float32)
    first_normalized, first_centered_scaled, first_inverse_deviation = layer_norm_forward(input_tokens, layer_norm_gain[0], layer_norm_bias[0])
    low1 = first_normalized.astype(jnp.bfloat16)
    proj = product('td,idc->itc', low1, w_qkv)
    query = (proj[0] + b_qv[0]).astype(jnp.bfloat16)
    key_rows = proj[1].astype(jnp.bfloat16)
    value = (proj[2] + b_qv[1]).astype(jnp.bfloat16)
    heads_out, logsum = attend(query, key_rows, value, allowed)
    first_hidden_state = input_tokens + jnp.dot(heads_out, w_out.T, preferred_element_type=jnp.float32) + b_out
    second_normalized, second_centered_scaled, second_inverse_deviation = layer_norm_forward(first_hidden_state, layer_norm_gain[1], layer_norm_bias[1])
    low2 = second_normalized.astype(jnp.bfloat16)
    pre_act = jnp.dot(low2, w_fc1, preferred_element_type=jnp.float32) + b_fc1
    act, slope = gelu_parts(pre_act)
    act_low = act.astype(jnp.bfloat16)
    result = first_hidden_state + jnp.dot(act_low, w_fc2.T, preferred_element_type=jnp.float32) + b_fc2
    output = jnp.where(live_rows[:, None], result, 0.0).astype(jnp.bfloat16)
    grad_y = jnp.where(live_rows[:, None], block_cot, jnp.zeros_like(block_cot))
    flat_output_gradient = grad_y.astype(jnp.float32)
    d_pre = (jnp.dot(grad_y, w_fc2, preferred_element_type=jnp.float32) * slope).astype(jnp.bfloat16)
    g_fc2 = jnp.dot(grad_y.T, act_low, preferred_element_type=jnp.float32)
    g_bfc2 = lax.optimization_barrier(jnp.sum(flat_output_gradient, axis=0))
    g_fc1 = jnp.dot(low2.T, d_pre, preferred_element_type=jnp.float32)
    g_bfc1 = lax.optimization_barrier(jnp.sum(d_pre.astype(jnp.float32), axis=0))
    second_norm_delta = jnp.dot(d_pre, w_fc1.T, preferred_element_type=jnp.float32)
    second_gain_gradient = lax.optimization_barrier(jnp.sum(second_norm_delta * second_centered_scaled, axis=0))
    g_shift2 = lax.optimization_barrier(jnp.sum(second_norm_delta, axis=0))
    hidden_first_gradient = flat_output_gradient + layer_norm_backward(second_norm_delta, layer_norm_gain[1], second_centered_scaled, second_inverse_deviation)
    grad_low = hidden_first_gradient.astype(jnp.bfloat16)
    g_out = jnp.dot(grad_low.T, heads_out, preferred_element_type=jnp.float32)
    g_bout = lax.optimization_barrier(jnp.sum(hidden_first_gradient, axis=0))
    d_heads = jnp.dot(grad_low, w_out, preferred_element_type=jnp.float32).astype(jnp.bfloat16)
    d_query, d_key, d_value = attend_back(query, key_rows, value, heads_out, d_heads, logsum, allowed)
    stacked = jnp.stack([d_query, d_key, d_value])
    g_qkv = product('td,itc->idc', low1, stacked)
    g_bqv = jnp.stack([lax.optimization_barrier(jnp.sum(d_query.astype(jnp.float32), axis=0)), lax.optimization_barrier(jnp.sum(d_value.astype(jnp.float32), axis=0))])
    first_norm_delta = product('itc,idc->td', stacked, w_qkv)
    first_gain_gradient = lax.optimization_barrier(jnp.sum(first_norm_delta * first_centered_scaled, axis=0))
    g_shift1 = lax.optimization_barrier(jnp.sum(first_norm_delta, axis=0))
    input_gradient = hidden_first_gradient + layer_norm_backward(first_norm_delta, layer_norm_gain[0], first_centered_scaled, first_inverse_deviation)
    grads = (jnp.stack([first_gain_gradient, second_gain_gradient]), jnp.stack([g_shift1, g_shift2]), g_qkv, g_bqv, g_out, g_bout, g_fc1, g_bfc1, g_fc2, g_bfc2)
    return (output, input_gradient, grads)

def reference(tokens, cotangent, seq_lens, layer_norm_gain, layer_norm_bias, w_qkv, b_qv, w_out, b_out, w_fc1, b_fc1, w_fc2, b_fc2):
    block_ins = tokens.reshape(N_DP, TOK_DEV, D)
    block_cots = cotangent.reshape(N_DP, TOK_DEV, D)
    block_lens = seq_lens.reshape(N_DP, SEQ_DEV)
    zero_grads = (jnp.zeros((2, D), jnp.float32), jnp.zeros((2, D), jnp.float32), jnp.zeros((3, D, D), jnp.float32), jnp.zeros((2, D), jnp.float32), jnp.zeros((D, D), jnp.float32), jnp.zeros((D,), jnp.float32), jnp.zeros((D, FF), jnp.float32), jnp.zeros((FF,), jnp.float32), jnp.zeros((D, FF), jnp.float32), jnp.zeros((D,), jnp.float32))

    def step_block(carry, items):
        block_in, block_cot, lengths = items
        output, input_gradient, grads = one_block(block_in, block_cot, lengths, layer_norm_gain, layer_norm_bias, w_qkv, b_qv, w_out, b_out, w_fc1, b_fc1, w_fc2, b_fc2)
        carry = tuple((total + part for total, part in zip(carry, grads)))
        return (carry, (output, input_gradient))
    totals, (outputs, grad_ins) = lax.scan(step_block, zero_grads, (block_ins, block_cots, block_lens))
    return (outputs.reshape(TOKENS, D), grad_ins.reshape(TOKENS, D), totals[0], totals[1], totals[2], totals[3], totals[4], totals[5], totals[6], totals[7], totals[8], totals[9])
```

```python
import jax
import jax.numpy as jnp
from jax import lax
from jax.sharding import PartitionSpec as P

HEAD_DIM = 64


NORM_EPS = 1e-05
GELU_COEF = 0.7978845608028654


def product(spec, left, right):
    return jnp.einsum(spec, left, right, preferred_element_type=jnp.float32)


def seq_masks(lengths, row_count):
    ends = jnp.cumsum(lengths, dtype=jnp.int32)
    places = jnp.arange(row_count, dtype=jnp.int32)
    segment = jnp.sum((places[:, None] >= ends[None, :]).astype(jnp.int32), axis=1)
    allowed = (segment[:, None] == segment[None, :]) & (places[:, None] >= places[None, :])
    live_rows = places < ends[-1]
    return (allowed, live_rows)


def layer_norm_forward(hidden, gain, shift):
    center = hidden - jnp.mean(hidden, axis=-1, keepdims=True)
    inv_std = lax.rsqrt(jnp.mean(center * center, axis=-1, keepdims=True) + NORM_EPS)
    normal_x = center * inv_std
    return (normal_x * gain + shift, normal_x, inv_std)


def layer_norm_backward(grad_out, gain, normal_x, inv_std):
    scaled = grad_out * gain
    return inv_std * (
        scaled
        - jnp.mean(scaled, axis=-1, keepdims=True)
        - normal_x * jnp.mean(scaled * normal_x, axis=-1, keepdims=True)
    )


def gelu_parts(pre_act):
    inner = GELU_COEF * (pre_act + 0.044715 * pre_act * pre_act * pre_act)
    tanh_val = jnp.tanh(inner)
    value = 0.5 * pre_act * (1.0 + tanh_val)
    slope = 0.5 * (1.0 + tanh_val) + 0.5 * pre_act * (1.0 - tanh_val * tanh_val) * GELU_COEF * (
        1.0 + 3.0 * 0.044715 * pre_act * pre_act
    )
    return (value, slope)


def split_heads(matrix):
    return matrix.reshape(matrix.shape[0], matrix.shape[1] // HEAD_DIM, HEAD_DIM)


def head_scores(query, key_rows, allowed):
    scores = product("qhd,khd->hqk", split_heads(query), split_heads(key_rows)) * HEAD_DIM ** (-0.5)
    return jnp.where(allowed[None], scores, -1e30)


def attend(query, key_rows, value, allowed):
    scores = head_scores(query, key_rows, allowed)
    row_max = jnp.max(scores, axis=-1, keepdims=True)
    logsum = row_max + jnp.log(jnp.sum(jnp.exp(scores - row_max), axis=-1, keepdims=True))
    weights = jnp.exp(scores - logsum).astype(jnp.bfloat16)
    mixed = product("hqk,khd->qhd", weights, split_heads(value)).astype(jnp.bfloat16)
    return (mixed.reshape(query.shape[0], -1), logsum)


def attend_back(query, key_rows, value, heads_out, d_heads, logsum, allowed):
    scores = head_scores(query, key_rows, allowed)
    probs = jnp.exp(scores - logsum)
    probs_low = probs.astype(jnp.bfloat16)
    d_split = split_heads(d_heads)
    d_prob = product("qhd,khd->hqk", d_split, split_heads(value))
    delta = jnp.sum(
        d_split.astype(jnp.float32) * split_heads(heads_out).astype(jnp.float32), axis=-1
    )
    d_score = (probs * (d_prob - jnp.transpose(delta)[:, :, None]) * HEAD_DIM ** (-0.5)).astype(
        jnp.bfloat16
    )
    d_query = product("hqk,khd->qhd", d_score, split_heads(key_rows)).astype(jnp.bfloat16)
    d_key = product("hqk,qhd->khd", d_score, split_heads(query)).astype(jnp.bfloat16)
    d_value = product("hqk,qhd->khd", probs_low, d_split).astype(jnp.bfloat16)
    row_count = query.shape[0]
    return (
        d_query.reshape(row_count, -1),
        d_key.reshape(row_count, -1),
        d_value.reshape(row_count, -1),
    )


def sum_tensor(part):
    low = lax.optimization_barrier(part.astype(jnp.bfloat16))
    count = lax.axis_size("tensor")
    if count != 2:
        return lax.psum(low, "tensor").astype(jnp.float32)
    other = lax.ppermute(low, "tensor", [(0, 1), (1, 0)])
    return low.astype(jnp.float32) + other.astype(jnp.float32)


def sum_dp(vectors):
    return lax.psum(vectors, "dp")


def body(
    tokens,
    cotangent,
    seq_lens,
    layer_norm_gain,
    layer_norm_bias,
    w_qkv,
    b_qv,
    w_out,
    b_out,
    w_fc1,
    b_fc1,
    w_fc2,
    b_fc2,
):
    heads_width, hidden_width = w_out.shape[1], w_fc1.shape[1]
    attn_shards = jnp.concatenate([w_qkv[0], w_qkv[1], w_qkv[2], w_out], axis=1)
    mlp_shards = jnp.concatenate([w_fc1, w_fc2], axis=1)
    attn_full = lax.all_gather(attn_shards, "dp", axis=0, tiled=True)
    mlp_full = lax.all_gather(mlp_shards, "dp", axis=0, tiled=True)
    qkv_full, out_full = attn_full[:, : 3 * heads_width], attn_full[:, 3 * heads_width :]
    fc1_full, fc2_full = mlp_full[:, :hidden_width], mlp_full[:, hidden_width:]
    allowed, live_rows = seq_masks(seq_lens, tokens.shape[0])
    input_tokens = tokens.astype(jnp.float32)
    first_normalized, first_centered_scaled, first_inverse_deviation = layer_norm_forward(
        input_tokens, layer_norm_gain[0], layer_norm_bias[0]
    )
    low1 = first_normalized.astype(jnp.bfloat16)
    proj = product("td,dc->tc", low1, qkv_full)
    query = (proj[:, :heads_width] + b_qv[0]).astype(jnp.bfloat16)
    key_rows = proj[:, heads_width : 2 * heads_width].astype(jnp.bfloat16)
    value = (proj[:, 2 * heads_width :] + b_qv[1]).astype(jnp.bfloat16)
    heads_out, logsum = attend(query, key_rows, value, allowed)
    attn_part = product("tc,dc->td", heads_out, out_full)
    attn_mix = sum_tensor(attn_part)
    first_hidden_state = input_tokens + attn_mix + b_out
    second_normalized, second_centered_scaled, second_inverse_deviation = layer_norm_forward(
        first_hidden_state, layer_norm_gain[1], layer_norm_bias[1]
    )
    low2 = second_normalized.astype(jnp.bfloat16)
    pre_act = jnp.dot(low2, fc1_full, preferred_element_type=jnp.float32) + b_fc1
    act, slope = gelu_parts(pre_act)
    act_low = act.astype(jnp.bfloat16)
    mlp_part = product("tf,df->td", act_low, fc2_full)
    mlp_mix = sum_tensor(mlp_part)
    result = first_hidden_state + mlp_mix + b_fc2
    output = jnp.where(live_rows[:, None], result, 0.0).astype(jnp.bfloat16)
    qkv_back, out_back, fc1_back, fc2_back = (qkv_full, out_full, fc1_full, fc2_full)
    grad_y = jnp.where(live_rows[:, None], cotangent, jnp.zeros_like(cotangent))
    flat_output_gradient = grad_y.astype(jnp.float32)
    d_pre = (jnp.dot(grad_y, fc2_back, preferred_element_type=jnp.float32) * slope).astype(
        jnp.bfloat16
    )
    g_fc2 = product("td,tf->df", grad_y, act_low)
    g_bfc2 = jnp.sum(flat_output_gradient, axis=0)
    g_fc1 = product("td,tf->df", low2, d_pre)
    g_mlp = jnp.concatenate([g_fc1.astype(jnp.bfloat16), g_fc2.astype(jnp.bfloat16)], axis=1)
    shard_mlp = lax.psum_scatter(g_mlp, "dp", scatter_dimension=0, tiled=True)
    g_bfc1 = jnp.sum(d_pre.astype(jnp.float32), axis=0)
    d_norm2_part = product("tf,df->td", d_pre, fc1_back)
    second_norm_delta = sum_tensor(d_norm2_part)
    second_gain_gradient = jnp.sum(second_norm_delta * second_centered_scaled, axis=0)
    g_shift2 = jnp.sum(second_norm_delta, axis=0)
    hidden_first_gradient = flat_output_gradient + layer_norm_backward(
        second_norm_delta, layer_norm_gain[1], second_centered_scaled, second_inverse_deviation
    )
    grad_low = hidden_first_gradient.astype(jnp.bfloat16)
    g_out = product("td,tc->dc", grad_low, heads_out)
    g_bout = jnp.sum(hidden_first_gradient, axis=0)
    d_heads = jnp.dot(grad_low, out_back, preferred_element_type=jnp.float32).astype(jnp.bfloat16)
    d_query, d_key, d_value = attend_back(
        query, key_rows, value, heads_out, d_heads, logsum, allowed
    )
    stacked = jnp.concatenate([d_query, d_key, d_value], axis=1)
    g_qkv = product("td,tc->dc", low1, stacked)
    g_attn = jnp.concatenate([g_qkv.astype(jnp.bfloat16), g_out.astype(jnp.bfloat16)], axis=1)
    shard_attn = lax.psum_scatter(g_attn, "dp", scatter_dimension=0, tiled=True)
    g_bqv = jnp.stack(
        [jnp.sum(d_query.astype(jnp.float32), axis=0), jnp.sum(d_value.astype(jnp.float32), axis=0)]
    )
    d_norm1_part = product("tc,dc->td", stacked, qkv_back)
    first_norm_delta = sum_tensor(d_norm1_part)
    first_gain_gradient = jnp.sum(first_norm_delta * first_centered_scaled, axis=0)
    g_shift1 = jnp.sum(first_norm_delta, axis=0)
    input_gradient = hidden_first_gradient + layer_norm_backward(
        first_norm_delta, layer_norm_gain[0], first_centered_scaled, first_inverse_deviation
    )
    shard_attn, shard_mlp = shard_attn.astype(jnp.float32), shard_mlp.astype(jnp.float32)
    shard_qkv = jnp.stack([shard_attn[:, i * heads_width : (i + 1) * heads_width] for i in range(3)])
    shard_out = shard_attn[:, 3 * heads_width :]
    shard_fc1, shard_fc2 = shard_mlp[:, :hidden_width], shard_mlp[:, hidden_width:]
    vectors = jnp.concatenate(
        [
            first_gain_gradient,
            second_gain_gradient,
            g_shift1,
            g_shift2,
            g_bqv.reshape(-1),
            g_bout,
            g_bfc1,
            g_bfc2,
        ]
    )
    vectors = sum_dp(vectors)
    width = tokens.shape[1]
    cuts = [2 * width, 4 * width, 4 * width + 2 * heads_width]
    cuts += [cuts[-1] + width, cuts[-1] + width + hidden_width]
    gain_sum, shift_sum, bqv_sum, bout_sum, bfc1_sum, bfc2_sum = jnp.split(vectors, cuts)
    gain_sum, shift_sum = gain_sum.reshape(2, width), shift_sum.reshape(2, width)
    bqv_sum = bqv_sum.reshape(2, heads_width)
    return (
        output,
        input_gradient,
        gain_sum,
        shift_sum,
        shard_qkv,
        bqv_sum,
        shard_out,
        bout_sum,
        shard_fc1,
        bfc1_sum,
        shard_fc2,
        bfc2_sum,
    )


def solution(mesh):
    in_specs = (
        P("dp", None),
        P("dp", None),
        P("dp"),
        P(),
        P(),
        P(None, "dp", "tensor"),
        P(None, "tensor"),
        P("dp", "tensor"),
        P(),
        P("dp", "tensor"),
        P("tensor"),
        P("dp", "tensor"),
        P(),
    )
    out_specs = (
        P("dp", None),
        P("dp", None),
        P(),
        P(),
        P(None, "dp", "tensor"),
        P(None, "tensor"),
        P("dp", "tensor"),
        P(),
        P("dp", "tensor"),
        P("tensor"),
        P("dp", "tensor"),
        P(),
    )
    return jax.shard_map(body, mesh=mesh, in_specs=in_specs, out_specs=out_specs, check_vma=False)
```

```python
import jax
import jax.numpy as jnp
from jax import lax
from jax.experimental import pallas as pl
from jax.experimental.pallas import tpu as pltpu
from jax.sharding import PartitionSpec as P

HEAD_DIM = 64


NORM_EPS = 1e-05
GELU_COEF = 0.7978845608028654


def product(spec, left, right):
    return jnp.einsum(spec, left, right, preferred_element_type=jnp.float32)


def seq_masks(lengths, row_count):
    ends = jnp.cumsum(lengths, dtype=jnp.int32)
    places = jnp.arange(row_count, dtype=jnp.int32)
    segment = jnp.sum((places[:, None] >= ends[None, :]).astype(jnp.int32), axis=1)
    allowed = (segment[:, None] == segment[None, :]) & (places[:, None] >= places[None, :])
    live_rows = places < ends[-1]
    return (allowed, live_rows)


def layer_norm_forward(hidden, gain, shift):
    center = hidden - jnp.mean(hidden, axis=-1, keepdims=True)
    inv_std = lax.rsqrt(jnp.mean(center * center, axis=-1, keepdims=True) + NORM_EPS)
    normal_x = center * inv_std
    return (normal_x * gain + shift, normal_x, inv_std)


def layer_norm_backward(grad_out, gain, normal_x, inv_std):
    scaled = grad_out * gain
    return inv_std * (
        scaled
        - jnp.mean(scaled, axis=-1, keepdims=True)
        - normal_x * jnp.mean(scaled * normal_x, axis=-1, keepdims=True)
    )


def gelu_parts(pre_act):
    inner = GELU_COEF * (pre_act + 0.044715 * pre_act * pre_act * pre_act)
    tanh_val = jnp.tanh(inner)
    value = 0.5 * pre_act * (1.0 + tanh_val)
    slope = 0.5 * (1.0 + tanh_val) + 0.5 * pre_act * (1.0 - tanh_val * tanh_val) * GELU_COEF * (
        1.0 + 3.0 * 0.044715 * pre_act * pre_act
    )
    return (value, slope)


def split_heads(matrix):
    return matrix.reshape(matrix.shape[0], matrix.shape[1] // HEAD_DIM, HEAD_DIM)


def head_scores(query, key_rows, allowed):
    scores = product("qhd,khd->hqk", split_heads(query), split_heads(key_rows)) * HEAD_DIM ** (-0.5)
    return jnp.where(allowed[None], scores, -1e30)


def attend(query, key_rows, value, allowed):
    scores = head_scores(query, key_rows, allowed)
    row_max = jnp.max(scores, axis=-1, keepdims=True)
    logsum = row_max + jnp.log(jnp.sum(jnp.exp(scores - row_max), axis=-1, keepdims=True))
    weights = jnp.exp(scores - logsum).astype(jnp.bfloat16)
    mixed = product("hqk,khd->qhd", weights, split_heads(value)).astype(jnp.bfloat16)
    return (mixed.reshape(query.shape[0], -1), logsum)


def attend_back(query, key_rows, value, heads_out, d_heads, logsum, allowed):
    scores = head_scores(query, key_rows, allowed)
    probs = jnp.exp(scores - logsum)
    probs_low = probs.astype(jnp.bfloat16)
    d_split = split_heads(d_heads)
    d_prob = product("qhd,khd->hqk", d_split, split_heads(value))
    delta = jnp.sum(
        d_split.astype(jnp.float32) * split_heads(heads_out).astype(jnp.float32), axis=-1
    )
    d_score = (probs * (d_prob - jnp.transpose(delta)[:, :, None]) * HEAD_DIM ** (-0.5)).astype(
        jnp.bfloat16
    )
    d_query = product("hqk,khd->qhd", d_score, split_heads(key_rows)).astype(jnp.bfloat16)
    d_key = product("hqk,qhd->khd", d_score, split_heads(query)).astype(jnp.bfloat16)
    d_value = product("hqk,qhd->khd", probs_low, d_split).astype(jnp.bfloat16)
    row_count = query.shape[0]
    return (
        d_query.reshape(row_count, -1),
        d_key.reshape(row_count, -1),
        d_value.reshape(row_count, -1),
    )


def sum_tensor(part):
    low = lax.optimization_barrier(part.astype(jnp.bfloat16))
    count = lax.axis_size("tensor")
    if count != 2:
        return lax.psum(low, "tensor").astype(jnp.float32)
    other = lax.ppermute(low, "tensor", [(0, 1), (1, 0)])
    return low.astype(jnp.float32) + other.astype(jnp.float32)


def chip_at(place, chips):
    place = (place + chips) % chips
    back = place // (chips // 2)
    return 2 * (place * (1 - back) + (chips - 1 - place) * back) + back


def ring_place(chips):
    device = lax.axis_index("dp")
    core, chip = device % 2, device // 2
    column, row = chip % 2, chip // 2
    place = row * (1 - column) + (chips - 1 - row) * column
    return device, chip, core, place


def send(source, target, send_sem, recv_sem, device):
    return pltpu.make_async_remote_copy(
        src_ref=source,
        dst_ref=target,
        send_sem=send_sem,
        recv_sem=recv_sem,
        device_id={"dp": device},
        device_id_type=pl.DeviceIdType.MESH,
    )


def meet(devices):
    barrier = pltpu.get_barrier_semaphore()
    for device in devices:
        pl.semaphore_signal(
            barrier, inc=1, device_id={"dp": device}, device_id_type=pl.DeviceIdType.MESH
        )
    pl.semaphore_wait(barrier, len(devices))


def gather_kernel(chips, own, out, rs, rr, ls, lr, ps, pr, own_sem):
    device, chip, core, place = ring_place(chips)
    right = 2 * chip_at(place + 1, chips) + core
    left = 2 * chip_at(place - 1, chips) + core
    partner = 2 * chip + 1 - core
    meet((right, left, partner))
    top, width = chips // 2, own.shape[1]
    half = width // 2

    def block(step, whose, hop, side):
        at = out.at[2 * chip_at(place + step, chips) + whose]
        if hop < top:
            return at
        return at.at[:, pl.ds(side * half, half)]

    started = []

    def go(copy):
        copy.start()
        started.append(copy)

    go(send(own, out.at[device], rs.at[0], rr.at[0], right))
    go(send(own, out.at[device], ls.at[0], lr.at[0], left))
    go(send(own, out.at[device], ps.at[0], pr.at[0], partner))
    keep = pltpu.make_async_copy(own, out.at[device], own_sem)
    keep.start()
    passed = [block(0, 1 - core, 0, 0)]
    for hop in range(1, top + 1):
        for side, sign, s_sem, r_sem, onward in ((0, -1, rs, rr, right), (1, 1, ls, lr, left)):
            here = block(sign * hop, core, hop, side)
            send(here, here, s_sem.at[hop - 1], r_sem.at[hop - 1], onward).wait_recv()
            if hop < top:
                part = block(sign * hop, core, hop + 1, side)
                go(send(part, part, s_sem.at[hop], r_sem.at[hop], onward))
            slot = len(passed)
            go(send(here, here, ps.at[slot], pr.at[slot], partner))
            passed.append(block(sign * hop, 1 - core, hop, side))
    for slot, here in enumerate(passed):
        send(here, here, ps.at[slot], pr.at[slot], partner).wait_recv()
    for copy in started:
        copy.wait_send()
    keep.wait()


def gather_rows(shard):
    count = lax.axis_size("dp")
    chips = count // 2
    top = chips // 2
    dma = pltpu.SemaphoreType.DMA
    out = pl.pallas_call(
        lambda *refs: gather_kernel(chips, *refs),
        out_shape=jax.ShapeDtypeStruct((count, *shard.shape), shard.dtype),
        in_specs=[pl.BlockSpec(memory_space=pltpu.VMEM)],
        out_specs=pl.BlockSpec(memory_space=pl.ANY),
        scratch_shapes=[dma((top,))] * 4 + [dma((chips + 1,))] * 2 + [dma],
        compiler_params=pltpu.CompilerParams(collective_id=0, has_side_effects=True),
        name="gather_rows",
    )(shard)
    return out.reshape(count * shard.shape[0], shard.shape[1])


def scatter_kernel(
    chips, grads, vec, out, vec_out,
    pbuf, rbuf, lbuf, rstage, lstage, vpart, vslots,
    ps, pr, rs, rr, ls, lr, vps, vpr, vrs, vrr, vls, vlr,
):
    device, chip, core, place = ring_place(chips)
    right = 2 * chip_at(place + 1, chips) + core
    left = 2 * chip_at(place - 1, chips) + core
    partner = 2 * chip + 1 - core
    meet((right, left, partner))
    top, width = chips // 2, out.shape[1]
    half = width // 2
    low, high = pl.ds(0, half), pl.ds(half, half)
    started = []

    def go(copy):
        copy.start()
        started.append(copy)

    order = [top]
    for step in range(1, top):
        order += [top - step, step - top]
    order.append(0)
    go(send(vec, vpart, vps.at[0], vpr.at[0], partner))
    for slot, step in enumerate(order):
        mine = grads.at[2 * chip_at(place + step, chips) + 1 - core]
        go(send(mine, pbuf.at[slot], ps.at[slot], pr.at[slot], partner))

    def pair_sum(slot):
        spot = pbuf.at[slot]
        send(spot, spot, ps.at[slot], pr.at[slot], partner).wait_recv()
        mine = grads[2 * chip_at(place + order[slot], chips) + core]
        return mine.astype(jnp.float32) + pbuf[slot].astype(jnp.float32)

    def arrived(spot, s_sem, r_sem):
        send(spot, spot, s_sem, r_sem, partner).wait_recv()

    first = pair_sum(0).astype(jnp.bfloat16)
    rstage[0, :, :half] = first[:, :half]
    go(send(rstage.at[0, :, low], rbuf.at[0, :, low], rs.at[0], rr.at[0], right))
    lstage[0, :, half:] = first[:, half:]
    go(send(lstage.at[0, :, high], lbuf.at[0, :, high], ls.at[0], lr.at[0], left))
    arrived(vpart, vps.at[0], vpr.at[0])
    vslots[chip] = vec[...] + vpart[...]
    go(send(vslots.at[chip], vslots.at[chip], vrs.at[0], vrr.at[0], right))
    go(send(vslots.at[chip], vslots.at[chip], vls.at[0], vlr.at[0], left))
    for step in range(1, top):
        for side, buf, stage, s_sem, r_sem, onward in (
            (0, rbuf, rstage, rs, rr, right),
            (1, lbuf, lstage, ls, lr, left),
        ):
            total = pair_sum(2 * step - 1 + side)
            if step == 1:
                cols = (low, high)[side]
                arrived(buf.at[0, :, cols], s_sem.at[0], r_sem.at[0])
                more = buf[0, :, side * half : (side + 1) * half].astype(jnp.float32)
                if side == 0:
                    stage[step, :, :half] = (total[:, :half] + more).astype(jnp.bfloat16)
                    stage[step, :, half:] = total[:, half:].astype(jnp.bfloat16)
                else:
                    stage[step, :, :half] = total[:, :half].astype(jnp.bfloat16)
                    stage[step, :, half:] = (total[:, half:] + more).astype(jnp.bfloat16)
            else:
                arrived(buf.at[step - 1], s_sem.at[step - 1], r_sem.at[step - 1])
                stage[step] = (total + buf[step - 1].astype(jnp.float32)).astype(jnp.bfloat16)
            go(send(stage.at[step], buf.at[step], s_sem.at[step], r_sem.at[step], onward))
        spot = vslots.at[chip_at(place - step, chips)]
        arrived(spot, vrs.at[step - 1], vrr.at[step - 1])
        go(send(spot, spot, vrs.at[step], vrr.at[step], right))
        spot = vslots.at[chip_at(place + step, chips)]
        arrived(spot, vls.at[step - 1], vlr.at[step - 1])
        if step < top - 1:
            go(send(spot, spot, vls.at[step], vlr.at[step], left))
    spot = vslots.at[chip_at(place - top, chips)]
    arrived(spot, vrs.at[top - 1], vrr.at[top - 1])
    vec_out[...] = jnp.sum(vslots[...], axis=0)
    total = pair_sum(len(order) - 1)
    arrived(rbuf.at[top - 1], rs.at[top - 1], rr.at[top - 1])
    arrived(lbuf.at[top - 1], ls.at[top - 1], lr.at[top - 1])
    out[...] = total + rbuf[top - 1].astype(jnp.float32) + lbuf[top - 1].astype(jnp.float32)
    for copy in started:
        copy.wait_send()


def scatter_rows(grads, vectors):
    count = lax.axis_size("dp")
    chips = count // 2
    top = chips // 2
    rows, width = grads.shape[0] // count, grads.shape[1]
    lines = vectors.shape[0] // 128
    dma, vmem = pltpu.SemaphoreType.DMA, pl.BlockSpec(memory_space=pltpu.VMEM)
    block = (rows, width)
    shard, sums = pl.pallas_call(
        lambda *refs: scatter_kernel(chips, *refs),
        out_shape=(
            jax.ShapeDtypeStruct(block, jnp.float32),
            jax.ShapeDtypeStruct((lines, 128), jnp.float32),
        ),
        in_specs=[vmem, vmem],
        out_specs=(vmem, vmem),
        scratch_shapes=[pltpu.VMEM((chips, *block), jnp.bfloat16)]
        + [pltpu.VMEM((top, *block), jnp.bfloat16)] * 4
        + [pltpu.VMEM((lines, 128), jnp.float32), pltpu.VMEM((chips, lines, 128), jnp.float32)]
        + [dma((chips,))] * 2
        + [dma((top,))] * 4
        + [dma((1,))] * 2
        + [dma((top,))] * 4,
        compiler_params=pltpu.CompilerParams(collective_id=1, has_side_effects=True),
        name="scatter_rows",
    )(grads.reshape(count, rows, width), vectors.reshape(lines, 128))
    return shard, sums.reshape(-1)


def body(
    tokens,
    cotangent,
    seq_lens,
    layer_norm_gain,
    layer_norm_bias,
    w_qkv,
    b_qv,
    w_out,
    b_out,
    w_fc1,
    b_fc1,
    w_fc2,
    b_fc2,
):
    heads_width, hidden_width = w_out.shape[1], w_fc1.shape[1]
    attn_shards = jnp.concatenate([w_qkv[0], w_qkv[1], w_qkv[2], w_out], axis=1)
    mlp_shards = jnp.concatenate([w_fc1, w_fc2], axis=1)
    mlp_full = lax.all_gather(mlp_shards, "dp", axis=0, tiled=True)
    attn_full = gather_rows(attn_shards)
    qkv_full, out_full = attn_full[:, : 3 * heads_width], attn_full[:, 3 * heads_width :]
    fc1_full, fc2_full = mlp_full[:, :hidden_width], mlp_full[:, hidden_width:]
    allowed, live_rows = seq_masks(seq_lens, tokens.shape[0])
    input_tokens = tokens.astype(jnp.float32)
    first_normalized, first_centered_scaled, first_inverse_deviation = layer_norm_forward(
        input_tokens, layer_norm_gain[0], layer_norm_bias[0]
    )
    low1 = first_normalized.astype(jnp.bfloat16)
    proj = product("td,dc->tc", low1, qkv_full)
    query = (proj[:, :heads_width] + b_qv[0]).astype(jnp.bfloat16)
    key_rows = proj[:, heads_width : 2 * heads_width].astype(jnp.bfloat16)
    value = (proj[:, 2 * heads_width :] + b_qv[1]).astype(jnp.bfloat16)
    heads_out, logsum = attend(query, key_rows, value, allowed)
    attn_part = product("tc,dc->td", heads_out, out_full)
    attn_mix = sum_tensor(attn_part)
    first_hidden_state = input_tokens + attn_mix + b_out
    second_normalized, second_centered_scaled, second_inverse_deviation = layer_norm_forward(
        first_hidden_state, layer_norm_gain[1], layer_norm_bias[1]
    )
    low2 = second_normalized.astype(jnp.bfloat16)
    pre_act = jnp.dot(low2, fc1_full, preferred_element_type=jnp.float32) + b_fc1
    act, slope = gelu_parts(pre_act)
    act_low = act.astype(jnp.bfloat16)
    mlp_part = product("tf,df->td", act_low, fc2_full)
    mlp_mix = sum_tensor(mlp_part)
    result = first_hidden_state + mlp_mix + b_fc2
    output = jnp.where(live_rows[:, None], result, 0.0).astype(jnp.bfloat16)
    qkv_back, out_back, fc1_back, fc2_back = (qkv_full, out_full, fc1_full, fc2_full)
    grad_y = jnp.where(live_rows[:, None], cotangent, jnp.zeros_like(cotangent))
    flat_output_gradient = grad_y.astype(jnp.float32)
    d_pre = (jnp.dot(grad_y, fc2_back, preferred_element_type=jnp.float32) * slope).astype(
        jnp.bfloat16
    )
    g_fc2 = product("td,tf->df", grad_y, act_low)
    g_bfc2 = jnp.sum(flat_output_gradient, axis=0)
    g_fc1 = product("td,tf->df", low2, d_pre)
    g_mlp = jnp.concatenate([g_fc1.astype(jnp.bfloat16), g_fc2.astype(jnp.bfloat16)], axis=1)
    shard_mlp = lax.psum_scatter(g_mlp, "dp", scatter_dimension=0, tiled=True)
    g_bfc1 = jnp.sum(d_pre.astype(jnp.float32), axis=0)
    d_norm2_part = product("tf,df->td", d_pre, fc1_back)
    second_norm_delta = sum_tensor(d_norm2_part)
    second_gain_gradient = jnp.sum(second_norm_delta * second_centered_scaled, axis=0)
    g_shift2 = jnp.sum(second_norm_delta, axis=0)
    hidden_first_gradient = flat_output_gradient + layer_norm_backward(
        second_norm_delta, layer_norm_gain[1], second_centered_scaled, second_inverse_deviation
    )
    grad_low = hidden_first_gradient.astype(jnp.bfloat16)
    g_out = product("td,tc->dc", grad_low, heads_out)
    g_bout = jnp.sum(hidden_first_gradient, axis=0)
    d_heads = jnp.dot(grad_low, out_back, preferred_element_type=jnp.float32).astype(jnp.bfloat16)
    d_query, d_key, d_value = attend_back(
        query, key_rows, value, heads_out, d_heads, logsum, allowed
    )
    stacked = jnp.concatenate([d_query, d_key, d_value], axis=1)
    g_qkv = product("td,tc->dc", low1, stacked)
    g_attn = jnp.concatenate([g_qkv.astype(jnp.bfloat16), g_out.astype(jnp.bfloat16)], axis=1)
    g_bqv = jnp.stack(
        [jnp.sum(d_query.astype(jnp.float32), axis=0), jnp.sum(d_value.astype(jnp.float32), axis=0)]
    )
    d_norm1_part = product("tc,dc->td", stacked, qkv_back)
    first_norm_delta = sum_tensor(d_norm1_part)
    first_gain_gradient = jnp.sum(first_norm_delta * first_centered_scaled, axis=0)
    g_shift1 = jnp.sum(first_norm_delta, axis=0)
    input_gradient = hidden_first_gradient + layer_norm_backward(
        first_norm_delta, layer_norm_gain[0], first_centered_scaled, first_inverse_deviation
    )
    shard_mlp = shard_mlp.astype(jnp.float32)
    shard_fc1, shard_fc2 = shard_mlp[:, :hidden_width], shard_mlp[:, hidden_width:]
    vectors = jnp.concatenate(
        [
            first_gain_gradient,
            second_gain_gradient,
            g_shift1,
            g_shift2,
            g_bqv.reshape(-1),
            g_bout,
            g_bfc1,
            g_bfc2,
        ]
    )
    shard_attn, vectors = scatter_rows(g_attn, vectors)
    shard_qkv = jnp.stack([shard_attn[:, i * heads_width : (i + 1) * heads_width] for i in range(3)])
    shard_out = shard_attn[:, 3 * heads_width :]
    width = tokens.shape[1]
    cuts = [2 * width, 4 * width, 4 * width + 2 * heads_width]
    cuts += [cuts[-1] + width, cuts[-1] + width + hidden_width]
    gain_sum, shift_sum, bqv_sum, bout_sum, bfc1_sum, bfc2_sum = jnp.split(vectors, cuts)
    gain_sum, shift_sum = gain_sum.reshape(2, width), shift_sum.reshape(2, width)
    bqv_sum = bqv_sum.reshape(2, heads_width)
    return (
        output,
        input_gradient,
        gain_sum,
        shift_sum,
        shard_qkv,
        bqv_sum,
        shard_out,
        bout_sum,
        shard_fc1,
        bfc1_sum,
        shard_fc2,
        bfc2_sum,
    )


def solution(mesh):
    in_specs = (
        P("dp", None),
        P("dp", None),
        P("dp"),
        P(),
        P(),
        P(None, "dp", "tensor"),
        P(None, "tensor"),
        P("dp", "tensor"),
        P(),
        P("dp", "tensor"),
        P("tensor"),
        P("dp", "tensor"),
        P(),
    )
    out_specs = (
        P("dp", None),
        P("dp", None),
        P(),
        P(),
        P(None, "dp", "tensor"),
        P(None, "tensor"),
        P("dp", "tensor"),
        P(),
        P("dp", "tensor"),
        P("tensor"),
        P("dp", "tensor"),
        P(),
    )
    return jax.shard_map(body, mesh=mesh, in_specs=in_specs, out_specs=out_specs, check_vma=False)
```

```python
import jax
import jax.numpy as jnp
from jax import lax
from jax.experimental import pallas as pl
from jax.experimental.pallas import tpu as pltpu
from jax.sharding import PartitionSpec as P

HEAD_DIM = 64


NORM_EPS = 1e-05
GELU_COEF = 0.7978845608028654


def product(spec, left, right):
    return jnp.einsum(spec, left, right, preferred_element_type=jnp.float32)


def seq_masks(lengths, row_count):
    ends = jnp.cumsum(lengths, dtype=jnp.int32)
    places = jnp.arange(row_count, dtype=jnp.int32)
    segment = jnp.sum((places[:, None] >= ends[None, :]).astype(jnp.int32), axis=1)
    allowed = (segment[:, None] == segment[None, :]) & (places[:, None] >= places[None, :])
    live_rows = places < ends[-1]
    return (allowed, live_rows)


def layer_norm_forward(hidden, gain, shift):
    center = hidden - jnp.mean(hidden, axis=-1, keepdims=True)
    inv_std = lax.rsqrt(jnp.mean(center * center, axis=-1, keepdims=True) + NORM_EPS)
    normal_x = center * inv_std
    return (normal_x * gain + shift, normal_x, inv_std)


def layer_norm_backward(grad_out, gain, normal_x, inv_std):
    scaled = grad_out * gain
    return inv_std * (
        scaled
        - jnp.mean(scaled, axis=-1, keepdims=True)
        - normal_x * jnp.mean(scaled * normal_x, axis=-1, keepdims=True)
    )


def gelu_parts(pre_act):
    inner = GELU_COEF * (pre_act + 0.044715 * pre_act * pre_act * pre_act)
    tanh_val = jnp.tanh(inner)
    value = 0.5 * pre_act * (1.0 + tanh_val)
    slope = 0.5 * (1.0 + tanh_val) + 0.5 * pre_act * (1.0 - tanh_val * tanh_val) * GELU_COEF * (
        1.0 + 3.0 * 0.044715 * pre_act * pre_act
    )
    return (value, slope)


def split_heads(matrix):
    return matrix.reshape(matrix.shape[0], matrix.shape[1] // HEAD_DIM, HEAD_DIM)


def head_scores(query, key_rows, allowed):
    scores = product("qhd,khd->hqk", split_heads(query), split_heads(key_rows)) * HEAD_DIM ** (-0.5)
    return jnp.where(allowed[None], scores, -1e30)


def attend(query, key_rows, value, allowed):
    scores = head_scores(query, key_rows, allowed)
    row_max = jnp.max(scores, axis=-1, keepdims=True)
    logsum = row_max + jnp.log(jnp.sum(jnp.exp(scores - row_max), axis=-1, keepdims=True))
    weights = jnp.exp(scores - logsum).astype(jnp.bfloat16)
    mixed = product("hqk,khd->qhd", weights, split_heads(value)).astype(jnp.bfloat16)
    return (mixed.reshape(query.shape[0], -1), logsum)


def attend_back(query, key_rows, value, heads_out, d_heads, logsum, allowed):
    scores = head_scores(query, key_rows, allowed)
    probs = jnp.exp(scores - logsum)
    probs_low = probs.astype(jnp.bfloat16)
    d_split = split_heads(d_heads)
    d_prob = product("qhd,khd->hqk", d_split, split_heads(value))
    delta = jnp.sum(
        d_split.astype(jnp.float32) * split_heads(heads_out).astype(jnp.float32), axis=-1
    )
    d_score = (probs * (d_prob - jnp.transpose(delta)[:, :, None]) * HEAD_DIM ** (-0.5)).astype(
        jnp.bfloat16
    )
    d_query = product("hqk,khd->qhd", d_score, split_heads(key_rows)).astype(jnp.bfloat16)
    d_key = product("hqk,qhd->khd", d_score, split_heads(query)).astype(jnp.bfloat16)
    d_value = product("hqk,qhd->khd", probs_low, d_split).astype(jnp.bfloat16)
    row_count = query.shape[0]
    return (
        d_query.reshape(row_count, -1),
        d_key.reshape(row_count, -1),
        d_value.reshape(row_count, -1),
    )


def sum_tensor(part):
    low = lax.optimization_barrier(part.astype(jnp.bfloat16))
    count = lax.axis_size("tensor")
    if count != 2:
        return lax.psum(low, "tensor").astype(jnp.float32)
    other = lax.ppermute(low, "tensor", [(0, 1), (1, 0)])
    return low.astype(jnp.float32) + other.astype(jnp.float32)


def chip_at(place, chips):
    place = (place + chips) % chips
    back = place // (chips // 2)
    return 2 * (place * (1 - back) + (chips - 1 - place) * back) + back


def ring_place(chips):
    device = lax.axis_index("dp")
    core, chip = device % 2, device // 2
    column, row = chip % 2, chip // 2
    place = row * (1 - column) + (chips - 1 - row) * column
    return device, chip, core, place


def send(source, target, send_sem, recv_sem, device):
    return pltpu.make_async_remote_copy(
        src_ref=source,
        dst_ref=target,
        send_sem=send_sem,
        recv_sem=recv_sem,
        device_id={"dp": device},
        device_id_type=pl.DeviceIdType.MESH,
    )


def meet(devices):
    barrier = pltpu.get_barrier_semaphore()
    for device in devices:
        pl.semaphore_signal(
            barrier, inc=1, device_id={"dp": device}, device_id_type=pl.DeviceIdType.MESH
        )
    pl.semaphore_wait(barrier, len(devices))


def gather_kernel(chips, own, out, rs, rr, ls, lr, ps, pr, own_sem):
    device, chip, core, place = ring_place(chips)
    right = 2 * chip_at(place + 1, chips) + core
    left = 2 * chip_at(place - 1, chips) + core
    partner = 2 * chip + 1 - core
    meet((right, left, partner))
    top, width = chips // 2, own.shape[1]
    half = width // 2

    def block(step, whose, hop, side):
        at = out.at[2 * chip_at(place + step, chips) + whose]
        if hop < top:
            return at
        return at.at[:, pl.ds(side * half, half)]

    started = []

    def go(copy):
        copy.start()
        started.append(copy)

    go(send(own, out.at[device], rs.at[0], rr.at[0], right))
    go(send(own, out.at[device], ls.at[0], lr.at[0], left))
    go(send(own, out.at[device], ps.at[0], pr.at[0], partner))
    keep = pltpu.make_async_copy(own, out.at[device], own_sem)
    keep.start()
    passed = [block(0, 1 - core, 0, 0)]
    for hop in range(1, top + 1):
        for side, sign, s_sem, r_sem, onward in ((0, -1, rs, rr, right), (1, 1, ls, lr, left)):
            here = block(sign * hop, core, hop, side)
            send(here, here, s_sem.at[hop - 1], r_sem.at[hop - 1], onward).wait_recv()
            if hop < top:
                part = block(sign * hop, core, hop + 1, side)
                go(send(part, part, s_sem.at[hop], r_sem.at[hop], onward))
            slot = len(passed)
            go(send(here, here, ps.at[slot], pr.at[slot], partner))
            passed.append(block(sign * hop, 1 - core, hop, side))
    for slot, here in enumerate(passed):
        send(here, here, ps.at[slot], pr.at[slot], partner).wait_recv()
    for copy in started:
        copy.wait_send()
    keep.wait()


def gather_rows(shard):
    count = lax.axis_size("dp")
    chips = count // 2
    top = chips // 2
    dma = pltpu.SemaphoreType.DMA
    out = pl.pallas_call(
        lambda *refs: gather_kernel(chips, *refs),
        out_shape=jax.ShapeDtypeStruct((count, *shard.shape), shard.dtype),
        in_specs=[pl.BlockSpec(memory_space=pltpu.VMEM)],
        out_specs=pl.BlockSpec(memory_space=pl.ANY),
        scratch_shapes=[dma((top,))] * 4 + [dma((chips + 1,))] * 2 + [dma],
        compiler_params=pltpu.CompilerParams(collective_id=0, has_side_effects=True),
        name="gather_rows",
    )(shard)
    return out.reshape(count * shard.shape[0], shard.shape[1])


def scatter_kernel(
    chips, parts, vec, out, vec_out,
    pbuf, rbuf, lbuf, rstage, lstage, vpart, vslots,
    ps, pr, rs, rr, ls, lr, vps, vpr, vrs, vrr, vls, vlr,
):
    device, chip, core, place = ring_place(chips)
    right = 2 * chip_at(place + 1, chips) + core
    left = 2 * chip_at(place - 1, chips) + core
    partner = 2 * chip + 1 - core
    meet((right, left, partner))
    top, width = chips // 2, out.shape[1]
    half = width // 2
    low, high = pl.ds(0, half), pl.ds(half, half)
    started = []

    def go(copy):
        copy.start()
        started.append(copy)

    order = [top]
    for step in range(1, top):
        order += [top - step, step - top]
    order.append(0)
    go(send(vec, vpart, vps.at[0], vpr.at[0], partner))
    spans, edge = [], 0
    for part in parts:
        spans.append(pl.ds(edge, part.shape[2]))
        edge += part.shape[2]
    for slot, step in enumerate(order):
        theirs = 2 * chip_at(place + step, chips) + 1 - core
        for i, (part, span) in enumerate(zip(parts, spans)):
            spot = pbuf.at[slot, :, span]
            go(send(part.at[theirs], spot, ps.at[i, slot], pr.at[i, slot], partner))

    def pair_sum(slot):
        for i, span in enumerate(spans):
            spot = pbuf.at[slot, :, span]
            send(spot, spot, ps.at[i, slot], pr.at[i, slot], partner).wait_recv()
        ours = 2 * chip_at(place + order[slot], chips) + core
        mine = jnp.concatenate([part[ours] for part in parts], axis=1)
        return mine.astype(jnp.float32) + pbuf[slot].astype(jnp.float32)

    def arrived(spot, s_sem, r_sem):
        send(spot, spot, s_sem, r_sem, partner).wait_recv()

    first = pair_sum(0).astype(jnp.bfloat16)
    rstage[0, :, :half] = first[:, :half]
    go(send(rstage.at[0, :, low], rbuf.at[0, :, low], rs.at[0], rr.at[0], right))
    lstage[0, :, half:] = first[:, half:]
    go(send(lstage.at[0, :, high], lbuf.at[0, :, high], ls.at[0], lr.at[0], left))
    arrived(vpart, vps.at[0], vpr.at[0])
    vslots[chip] = vec[...] + vpart[...]
    go(send(vslots.at[chip], vslots.at[chip], vrs.at[0], vrr.at[0], right))
    go(send(vslots.at[chip], vslots.at[chip], vls.at[0], vlr.at[0], left))
    for step in range(1, top):
        for side, buf, stage, s_sem, r_sem, onward in (
            (0, rbuf, rstage, rs, rr, right),
            (1, lbuf, lstage, ls, lr, left),
        ):
            total = pair_sum(2 * step - 1 + side)
            if step == 1:
                cols = (low, high)[side]
                arrived(buf.at[0, :, cols], s_sem.at[0], r_sem.at[0])
                more = buf[0, :, side * half : (side + 1) * half].astype(jnp.float32)
                if side == 0:
                    stage[step, :, :half] = (total[:, :half] + more).astype(jnp.bfloat16)
                    stage[step, :, half:] = total[:, half:].astype(jnp.bfloat16)
                else:
                    stage[step, :, :half] = total[:, :half].astype(jnp.bfloat16)
                    stage[step, :, half:] = (total[:, half:] + more).astype(jnp.bfloat16)
            else:
                arrived(buf.at[step - 1], s_sem.at[step - 1], r_sem.at[step - 1])
                stage[step] = (total + buf[step - 1].astype(jnp.float32)).astype(jnp.bfloat16)
            go(send(stage.at[step], buf.at[step], s_sem.at[step], r_sem.at[step], onward))
        spot = vslots.at[chip_at(place - step, chips)]
        arrived(spot, vrs.at[step - 1], vrr.at[step - 1])
        go(send(spot, spot, vrs.at[step], vrr.at[step], right))
        spot = vslots.at[chip_at(place + step, chips)]
        arrived(spot, vls.at[step - 1], vlr.at[step - 1])
        if step < top - 1:
            go(send(spot, spot, vls.at[step], vlr.at[step], left))
    spot = vslots.at[chip_at(place - top, chips)]
    arrived(spot, vrs.at[top - 1], vrr.at[top - 1])
    vec_out[...] = jnp.sum(vslots[...], axis=0)
    total = pair_sum(len(order) - 1)
    arrived(rbuf.at[top - 1], rs.at[top - 1], rr.at[top - 1])
    arrived(lbuf.at[top - 1], ls.at[top - 1], lr.at[top - 1])
    out[...] = total + rbuf[top - 1].astype(jnp.float32) + lbuf[top - 1].astype(jnp.float32)
    for copy in started:
        copy.wait_send()


def scatter_rows(grads, vectors):
    count = lax.axis_size("dp")
    chips = count // 2
    top = chips // 2
    rows, width = grads[0].shape[0] // count, sum(part.shape[1] for part in grads)
    amount = len(grads)
    lines = vectors.shape[0] // 128
    dma, vmem = pltpu.SemaphoreType.DMA, pl.BlockSpec(memory_space=pltpu.VMEM)
    block = (rows, width)
    shard, sums = pl.pallas_call(
        lambda *refs: scatter_kernel(chips, refs[:amount], *refs[amount:]),
        out_shape=(
            jax.ShapeDtypeStruct(block, jnp.float32),
            jax.ShapeDtypeStruct((lines, 128), jnp.float32),
        ),
        in_specs=[vmem] * (amount + 1),
        out_specs=(vmem, vmem),
        scratch_shapes=[pltpu.VMEM((chips, *block), jnp.bfloat16)]
        + [pltpu.VMEM((top, *block), jnp.bfloat16)] * 4
        + [pltpu.VMEM((lines, 128), jnp.float32), pltpu.VMEM((chips, lines, 128), jnp.float32)]
        + [dma((amount, chips))] * 2
        + [dma((top,))] * 4
        + [dma((1,))] * 2
        + [dma((top,))] * 4,
        compiler_params=pltpu.CompilerParams(collective_id=1, has_side_effects=True),
        name="scatter_rows",
    )(*[part.reshape(count, rows, -1) for part in grads], vectors.reshape(lines, 128))
    return shard, sums.reshape(-1)


def body(
    tokens,
    cotangent,
    seq_lens,
    layer_norm_gain,
    layer_norm_bias,
    w_qkv,
    b_qv,
    w_out,
    b_out,
    w_fc1,
    b_fc1,
    w_fc2,
    b_fc2,
):
    heads_width, hidden_width = w_out.shape[1], w_fc1.shape[1]
    attn_shards = jnp.concatenate([w_qkv[0], w_qkv[1], w_qkv[2], w_out], axis=1)
    mlp_shards = jnp.concatenate([w_fc1, w_fc2], axis=1)
    mlp_full = lax.all_gather(mlp_shards, "dp", axis=0, tiled=True)
    attn_full = gather_rows(attn_shards)
    qkv_full, out_full = attn_full[:, : 3 * heads_width], attn_full[:, 3 * heads_width :]
    fc1_full, fc2_full = mlp_full[:, :hidden_width], mlp_full[:, hidden_width:]
    allowed, live_rows = seq_masks(seq_lens, tokens.shape[0])
    input_tokens = tokens.astype(jnp.float32)
    first_normalized, first_centered_scaled, first_inverse_deviation = layer_norm_forward(
        input_tokens, layer_norm_gain[0], layer_norm_bias[0]
    )
    low1 = first_normalized.astype(jnp.bfloat16)
    proj = product("td,dc->tc", low1, qkv_full)
    query = (proj[:, :heads_width] + b_qv[0]).astype(jnp.bfloat16)
    key_rows = proj[:, heads_width : 2 * heads_width].astype(jnp.bfloat16)
    value = (proj[:, 2 * heads_width :] + b_qv[1]).astype(jnp.bfloat16)
    heads_out, logsum = attend(query, key_rows, value, allowed)
    attn_part = product("tc,dc->td", heads_out, out_full)
    attn_mix = sum_tensor(attn_part)
    first_hidden_state = input_tokens + attn_mix + b_out
    second_normalized, second_centered_scaled, second_inverse_deviation = layer_norm_forward(
        first_hidden_state, layer_norm_gain[1], layer_norm_bias[1]
    )
    low2 = second_normalized.astype(jnp.bfloat16)
    pre_act = jnp.dot(low2, fc1_full, preferred_element_type=jnp.float32) + b_fc1
    act, slope = gelu_parts(pre_act)
    act_low = act.astype(jnp.bfloat16)
    mlp_part = product("tf,df->td", act_low, fc2_full)
    qkv_back, out_back, fc1_back, fc2_back = (qkv_full, out_full, fc1_full, fc2_full)
    grad_y = jnp.where(live_rows[:, None], cotangent, jnp.zeros_like(cotangent))
    flat_output_gradient = grad_y.astype(jnp.float32)
    d_pre = (jnp.dot(grad_y, fc2_back, preferred_element_type=jnp.float32) * slope).astype(
        jnp.bfloat16
    )
    g_fc2 = product("td,tf->df", grad_y, act_low)
    g_bfc2 = jnp.sum(flat_output_gradient, axis=0)
    g_fc1 = product("td,tf->df", low2, d_pre)
    g_fc2 = g_fc2.astype(jnp.bfloat16)
    shard_fc2 = lax.psum_scatter(g_fc2, "dp", scatter_dimension=0, tiled=True)
    g_bfc1 = jnp.sum(d_pre.astype(jnp.float32), axis=0)
    d_norm2_part = product("tf,df->td", d_pre, fc1_back)
    mlp_low, second_norm_delta = lax.optimization_barrier(
        (mlp_part.astype(jnp.bfloat16), sum_tensor(d_norm2_part))
    )
    mlp_mix = sum_tensor(mlp_low)
    second_gain_gradient = jnp.sum(second_norm_delta * second_centered_scaled, axis=0)
    g_shift2 = jnp.sum(second_norm_delta, axis=0)
    hidden_first_gradient = flat_output_gradient + layer_norm_backward(
        second_norm_delta, layer_norm_gain[1], second_centered_scaled, second_inverse_deviation
    )
    grad_low = hidden_first_gradient.astype(jnp.bfloat16)
    g_out = product("td,tc->dc", grad_low, heads_out)
    g_bout = jnp.sum(hidden_first_gradient, axis=0)
    d_heads = jnp.dot(grad_low, out_back, preferred_element_type=jnp.float32).astype(jnp.bfloat16)
    d_query, d_key, d_value = attend_back(
        query, key_rows, value, heads_out, d_heads, logsum, allowed
    )
    mlp_mix, d_query = lax.optimization_barrier((mlp_mix, d_query))
    result = first_hidden_state + mlp_mix + b_fc2
    output = jnp.where(live_rows[:, None], result, 0.0).astype(jnp.bfloat16)
    stacked = jnp.concatenate([d_query, d_key, d_value], axis=1)
    g_qkv = product("td,tc->dc", low1, stacked)
    ring_grads = [part.astype(jnp.bfloat16) for part in (g_qkv, g_out, g_fc1)]
    g_bqv = jnp.stack(
        [jnp.sum(d_query.astype(jnp.float32), axis=0), jnp.sum(d_value.astype(jnp.float32), axis=0)]
    )
    d_norm1_part = product("tc,dc->td", stacked, qkv_back)
    first_norm_delta = sum_tensor(d_norm1_part)
    first_gain_gradient = jnp.sum(first_norm_delta * first_centered_scaled, axis=0)
    g_shift1 = jnp.sum(first_norm_delta, axis=0)
    input_gradient = hidden_first_gradient + layer_norm_backward(
        first_norm_delta, layer_norm_gain[0], first_centered_scaled, first_inverse_deviation
    )
    shard_fc2 = shard_fc2.astype(jnp.float32)
    vectors = jnp.concatenate(
        [
            first_gain_gradient,
            second_gain_gradient,
            g_shift1,
            g_shift2,
            g_bqv.reshape(-1),
            g_bout,
            g_bfc1,
            g_bfc2,
        ]
    )
    shard_ring, vectors = scatter_rows(ring_grads, vectors)
    shard_qkv = jnp.stack([shard_ring[:, i * heads_width : (i + 1) * heads_width] for i in range(3)])
    shard_out = shard_ring[:, 3 * heads_width : 4 * heads_width]
    shard_fc1 = shard_ring[:, 4 * heads_width :]
    width = tokens.shape[1]
    cuts = [2 * width, 4 * width, 4 * width + 2 * heads_width]
    cuts += [cuts[-1] + width, cuts[-1] + width + hidden_width]
    gain_sum, shift_sum, bqv_sum, bout_sum, bfc1_sum, bfc2_sum = jnp.split(vectors, cuts)
    gain_sum, shift_sum = gain_sum.reshape(2, width), shift_sum.reshape(2, width)
    bqv_sum = bqv_sum.reshape(2, heads_width)
    return (
        output,
        input_gradient,
        gain_sum,
        shift_sum,
        shard_qkv,
        bqv_sum,
        shard_out,
        bout_sum,
        shard_fc1,
        bfc1_sum,
        shard_fc2,
        bfc2_sum,
    )


def solution(mesh):
    in_specs = (
        P("dp", None),
        P("dp", None),
        P("dp"),
        P(),
        P(),
        P(None, "dp", "tensor"),
        P(None, "tensor"),
        P("dp", "tensor"),
        P(),
        P("dp", "tensor"),
        P("tensor"),
        P("dp", "tensor"),
        P(),
    )
    out_specs = (
        P("dp", None),
        P("dp", None),
        P(),
        P(),
        P(None, "dp", "tensor"),
        P(None, "tensor"),
        P("dp", "tensor"),
        P(),
        P("dp", "tensor"),
        P("tensor"),
        P("dp", "tensor"),
        P(),
    )
    return jax.shard_map(body, mesh=mesh, in_specs=in_specs, out_specs=out_specs, check_vma=False)
```
